32 devices in a mesh: groups: 2 (over x), seq: 16 (over z, y, core).
Axes of the slice: x: 2, y: 2, z: 4, core: 2. Of those that a mesh axis runs over, the one named last changes fastest.
Arguments:
- queries: bfloat16 [256, 2560], P(('groups', 'seq')), parts along dimension 0, may hold values from -160 to 160
- new_keys: bfloat16 [256, 2560], P(('groups', 'seq')), parts along dimension 0, may hold values from -7 to 7
- new_values: bfloat16 [256, 2560], P(('groups', 'seq')), parts along dimension 0, may hold values from -6 to 6
- cache_keys: bfloat16 [16384, 2560], P(('groups', 'seq')), parts along dimension 0, may hold values from -6 to 6
- cache_values: bfloat16 [16384, 2560], P(('groups', 'seq')), parts along dimension 0, may hold values from -6 to 6
- victims: int32 [32], P('groups'), parts along dimension 0, may hold values from 0 to 63, as said below
Outputs:
- attended: bfloat16 [256, 2560], P(('groups', 'seq')), parts along dimension 0
The draws below stay inside these ranges and needn't reach their ends.
There are 2 independent parts, one for each index of `groups`. The reference program is written for one: setup_inputs(seed, part) draws one part's arguments, and reference() takes and returns one part's arrays. A program takes and returns all parts, laid end to end along the dimension named above; each array names one. Nothing has to cross between parts.
Inputs may be any that keep to these rules, and one draw needn't show every extreme that they name: `victims`: 16 distinct block ids of the cache; the first and the last block are always among them.
All inputs are finite; a program needn't handle non-finite values.
Results may differ from the reference program's by a relative error of at most 0.01.
Values may be sent and summed in bfloat16 or wider, within the bound.
A program may use at most 128 MiB of HBM per device.

```python
import math
import jax
import jax.numpy as jnp
from jax import lax

H = 20
HD = 128
BLK = 128
TOK = 128
NBLK = 64
EVICT = 16


def drawn_pair(key):
    query_seed = jax.random.fold_in(key, 101)
    probe_seed = jax.random.fold_in(key, 202)
    columns = H * HD
    probe_rows = jax.random.truncated_normal(probe_seed, -6.0, 6.0, (TOK, columns), jnp.float32)
    query_rows = 3.0 * jax.random.truncated_normal(query_seed, -5.0, 5.0, (TOK, columns), jnp.float32)
    return (query_rows, probe_rows)


def draw_queries(key, part):
    return drawn_pair(key)[0].astype(jnp.bfloat16)


def draw_new_keys(key, part):
    return drawn_pair(key)[1].astype(jnp.bfloat16)


def draw_victims(key, part):
    middle = jax.random.permutation(jax.random.fold_in(key, 404), NBLK - 2).astype(jnp.int32) + 1
    ends = jnp.array([0, NBLK - 1]).astype(jnp.int32)
    chosen = jnp.concatenate([ends, middle[:EVICT - 2]])
    return jax.random.permutation(jax.random.fold_in(key, 505), chosen).astype(jnp.int32)


def block_levels(stream_key, extent, shards, smallest, top_value):
    def one(position, parts):
        steps = jax.random.uniform(jax.random.fold_in(jax.random.fold_in(stream_key, 6), position), (parts,), jnp.float32, smallest / len(shards), top_value / len(shards))
        return jnp.repeat(jnp.exp(steps), extent[position] // parts).reshape((-1,) + (1,) * (len(extent) - position - 1))

    factor_of = one(*shards[0])
    for cut in shards[1:]:
        factor_of = factor_of * one(*cut)
    return factor_of


def scatter_about(stream_key, dims, scale, reach, split=(), kind=jnp.bfloat16):
    values = jax.random.normal(stream_key, dims, jnp.float32) * scale
    if len(split) > 0:
        values = block_levels(stream_key, dims, split, -0.22, 0.18) * values
    return jnp.clip(values, min=-reach, max=reach).astype(kind)


def setup_inputs(seed: int = 0, part: int = 0) -> dict:
    streams_of = jax.random.split(jax.random.key(seed), 7)
    part_keys = jax.random.split(jax.random.fold_in(streams_of[6], part), 7)
    return {
        "queries": draw_queries(jax.random.fold_in(jax.random.fold_in(streams_of[6], part), 71), part),
        "new_keys": draw_new_keys(jax.random.fold_in(jax.random.fold_in(streams_of[6], part), 71), part),
        "new_values": scatter_about(part_keys[2], (TOK, H * HD), 1.0, 6.0, ((0, 16),)),
        "cache_keys": scatter_about(part_keys[3], (NBLK * BLK, H * HD), 1.0, 6.0, ((0, 16),)),
        "cache_values": scatter_about(part_keys[4], (NBLK * BLK, H * HD), 1.0, 6.0, ((0, 16),)),
        "victims": draw_victims(jax.random.fold_in(jax.random.fold_in(streams_of[6], part), 71), part),
    }


def similarity(query_cols, other):
    return lax.dot_general(query_cols, other, (((1,), (1,)), ((), ())), preferred_element_type=jnp.float32)

def reference(queries, new_keys, new_values, cache_keys, cache_values, victims):
    block_total = cache_keys.shape[0] // BLK
    evicted = jnp.zeros((block_total,), jnp.int32).at[victims].set(1)
    cache_live = jnp.repeat(evicted == 0, BLK)[None, :]
    scaling = 1.0 / math.sqrt(HD)

    def one_head(head):
        first_col = head * HD
        query_cols = lax.dynamic_slice_in_dim(queries, first_col, HD, 1)
        cached = similarity(query_cols, lax.dynamic_slice_in_dim(cache_keys, first_col, HD, 1)) * scaling
        cached = jnp.where(cache_live, cached, -1e+30)
        fresh_scores = similarity(query_cols, lax.dynamic_slice_in_dim(new_keys, first_col, HD, 1)) * scaling
        row_top = jnp.maximum(lax.optimization_barrier(jnp.max(cached, axis=1)), lax.optimization_barrier(jnp.max(fresh_scores, axis=1)))
        cached_exp = jnp.where(cache_live, jnp.exp(cached - row_top[:, None]), 0.0)
        fresh_exp = jnp.exp(fresh_scores - row_top[:, None])
        row_mass = lax.optimization_barrier(jnp.sum(cached_exp, axis=1)) + lax.optimization_barrier(jnp.sum(fresh_exp, axis=1))
        head_out = jnp.dot(cached_exp.astype(jnp.bfloat16), lax.dynamic_slice_in_dim(cache_values, first_col, HD, 1), preferred_element_type=jnp.float32)
        head_out = head_out + jnp.dot(fresh_exp.astype(jnp.bfloat16), lax.dynamic_slice_in_dim(new_values, first_col, HD, 1), preferred_element_type=jnp.float32)
        return head_out / row_mass[:, None]
    stacked = lax.map(one_head, jnp.arange(H, dtype=jnp.int32))
    return jnp.transpose(stacked, (1, 0, 2)).reshape(TOK, H * HD).astype(jnp.bfloat16)
```

```python
import functools
import math

import jax
import jax.numpy as jnp
from jax import lax
from jax.experimental import pallas as pl
from jax.experimental.pallas import tpu as pltpu
from jax.sharding import PartitionSpec as P

HD = 128
BLK = 128
LANES = 128
HALF = 32
ROW_TILE = 128


def factors(members):
    fc = 2 if members % 2 == 0 else 1
    rest = members // fc
    fa = rest
    for cand in range(1, rest + 1):
        if rest % cand == 0 and cand * cand >= rest:
            fa = cand
            break
    return fa, rest // fa, fc


def chunks_of(heads):
    for count in (4, 5, 2, 3):
        if heads % count == 0 and heads // count <= HALF:
            return count
    return 1 if heads <= HALF else heads


def kernel(
    dims, chunks, q_ref, nk_ref, nv_ref, vic_ref, ck_ref, cv_ref, o_ref,
    qall, kbuf, vbuf, acc, send_c, recv_c, send_b, recv_b, send_a, recv_a,
    load_sem, own_sem, gs_sem, gr_sem, rs_sem, rr_sem,
):
    fa, fb, fc = dims
    members = fa * fb * fc
    tok, columns = q_ref.shape
    heads = columns // HD
    hc = heads // chunks
    width = hc * HD
    wide = width + LANES
    rows = ck_ref.shape[0]
    keys = kbuf.shape[0]
    block_count = rows // BLK
    exponent = math.log2(math.e) / math.sqrt(HD)

    me = lax.axis_index("seq")
    c = lax.rem(me, fc)
    b = lax.rem(lax.div(me, fc), fb)
    a = lax.div(me, fc * fb)

    def index(a_, b_, c_):
        return (a_ * fb + b_) * fc + c_

    def slot(a_, b_, c_):
        return (c_ * fb + b_) * fa + a_

    a_peers = [lax.rem(a + d, fa) for d in range(1, fa)]
    b_peers = [lax.rem(b + d, fb) for d in range(1, fb)]
    c_peers = [lax.rem(c + d, fc) for d in range(1, fc)]
    devices = (
        [index(p, b, c) for p in a_peers]
        + [index(a, p, c) for p in b_peers]
        + [index(a, b, p) for p in c_peers]
    )
    na, nb, nc = fa - 1, fb - 1, fc - 1

    def cols(j):
        return pl.ds(j * width, width)

    def wcols(j):
        return pl.ds(j * wide, wide)

    barrier = pltpu.get_barrier_semaphore()
    for dev in devices:
        pl.semaphore_signal(
            barrier, inc=1, device_id={"seq": dev}, device_id_type=pl.DeviceIdType.MESH
        )

    loads = []
    for j in range(chunks):
        pair = (
            pltpu.make_async_copy(
                ck_ref.at[:, cols(j)], kbuf.at[pl.ds(0, rows), cols(j)], load_sem.at[j, 0]
            ),
            pltpu.make_async_copy(
                cv_ref.at[:, cols(j)], vbuf.at[pl.ds(0, rows), cols(j)], load_sem.at[j, 1]
            ),
        )
        loads.append(pair)
    own_slot = slot(a, b, c)
    own = pltpu.make_async_copy(q_ref, qall.at[own_slot], own_sem)
    own.start()

    def remote(src, dst, sems, recvs, j, k):
        return pltpu.make_async_remote_copy(
            src_ref=src,
            dst_ref=dst,
            send_sem=sems.at[j, k],
            recv_sem=recvs.at[j, k],
            device_id={"seq": devices[k]},
            device_id_type=pl.DeviceIdType.MESH,
        )

    pl.semaphore_wait(barrier, len(devices))

    gather_a = [
        [
            remote(q_ref.at[:, cols(j)], qall.at[own_slot, :, cols(j)], gs_sem, gr_sem, j, k)
            for k in range(na)
        ]
        for j in range(chunks)
    ]
    for j in range(chunks):
        for copy in gather_a[j]:
            copy.start()
    for pair in loads:
        pair[0].start()
        pair[1].start()

    pad16 = 2 * tok - tok
    for src, dst in ((nk_ref, kbuf), (nv_ref, vbuf)):
        fresh = src[...].astype(jnp.float32)
        dst[pl.ds(rows, 2 * tok), :] = jnp.concatenate(
            [fresh, jnp.zeros((pad16, columns), jnp.float32)], axis=0
        ).astype(jnp.bfloat16)
        dst[pl.ds(rows + 2 * tok, keys - rows - 2 * tok), :] = jnp.zeros(
            (keys - rows - 2 * tok, columns), jnp.bfloat16
        )

    victims = vic_ref[...]
    pieces = []
    for k in range(block_count):
        hit = jnp.where(victims == me * block_count + k, 1.0, 0.0)
        hit = jnp.max(hit, axis=1, keepdims=True)
        pieces.append(jnp.broadcast_to(hit, (1, BLK)) * -1e30)
    tail = lax.broadcasted_iota(jnp.int32, (1, keys - rows), 1)
    pieces.append(jnp.where(tail < tok, 0.0, -1e30))
    bias = jnp.concatenate(pieces, axis=1)

    def gather_b(j):
        src = qall.at[pl.ds(slot(0, b, c), fa), :, cols(j)]
        return [remote(src, src, gs_sem, gr_sem, j, na + k) for k in range(nb)]

    def gather_c(j):
        src = qall.at[pl.ds(slot(0, 0, c), fa * fb), :, cols(j)]
        return [remote(src, src, gs_sem, gr_sem, j, na + nb + k) for k in range(nc)]

    tile_slots = max(1, min(members, ROW_TILE // tok))
    tiles = members // tile_slots

    def lane_of(r):
        return lax.broadcasted_iota(jnp.int32, (r, LANES), 1)

    def compute(j):
        def tile(t):
            first = t * tile_slots
            r = tile_slots * tok
            lane = lane_of(r)

            def head(h, stats):
                col = pl.multiple_of(j * width + h * HD, HD)
                q = qall[pl.ds(first, tile_slots), :, pl.ds(col, HD)]
                q = q.astype(jnp.float32).reshape(r, HD).astype(jnp.bfloat16)
                s = lax.dot_general(
                    q, kbuf[:, pl.ds(col, HD)], (((1,), (1,)), ((), ())),
                    preferred_element_type=jnp.float32,
                )
                s = s * exponent + bias
                top = jnp.max(s, axis=1, keepdims=True)
                top = top.astype(jnp.bfloat16).astype(jnp.float32)
                e = jnp.exp2(s - top)
                mass = jnp.sum(e, axis=1, keepdims=True)
                out = jnp.dot(
                    e.astype(jnp.bfloat16), vbuf[:, pl.ds(col, HD)],
                    preferred_element_type=jnp.float32,
                )
                at = pl.multiple_of(j * wide + h * HD, HD)
                acc[pl.ds(first, tile_slots), :, pl.ds(at, HD)] = out.reshape(tile_slots, tok, HD)
                stats = jnp.where(lane == h, top, stats)
                return jnp.where(lane == h + HALF, mass, stats)

            stats = lax.fori_loop(
                0, hc, head, jnp.zeros((r, LANES), jnp.float32), unroll=tiles == 1
            )
            acc[pl.ds(first, tile_slots), :, pl.ds(j * wide + width, LANES)] = stats.reshape(
                tile_slots, tok, LANES
            )

        if tiles == 1:
            tile(0)
        else:
            pl.loop(0, tiles)(tile)

    def encode(stats):
        high = stats.astype(jnp.bfloat16).astype(jnp.float32)
        return (high + pltpu.roll(stats - high, HALF, 1)).astype(jnp.bfloat16)

    def decode(stats):
        low = pltpu.roll(stats, LANES - HALF, 1)
        return stats + jnp.where(lane_of(stats.shape[0]) < HALF, 0.0, low)

    def pack(first, count, buf, j):
        r = count * tok
        buf[:, :, cols_w(j, width)] = acc[pl.ds(first, count), :, cols_w(j, width)].astype(
            jnp.bfloat16
        )
        stats = acc[pl.ds(first, count), :, pl.ds(j * wide + width, LANES)].reshape(r, LANES)
        buf[:, :, pl.ds(j * wide + width, LANES)] = encode(stats).reshape(count, tok, LANES)

    def cols_w(j, w):
        return pl.ds(j * wide, w)

    def merge(first, count, parts, j, last=False):
        r = count * tok
        at = pl.ds(j * wide + width, LANES)
        lane = lane_of(r)
        stats = [acc[pl.ds(first, count), :, at].reshape(r, LANES)]
        for ref in parts:
            stats.append(decode(ref[:, :, at].astype(jnp.float32).reshape(r, LANES)))
        top = functools.reduce(jnp.maximum, stats)
        factor = [jnp.exp2(s - top) for s in stats]
        mass = sum(pltpu.roll(f, HALF, 1) * s for f, s in zip(factor, stats))
        if last:
            inverse = pltpu.roll(1.0 / jnp.where(lane < HALF, 1.0, mass), LANES - HALF, 1)
            factor = [f * inverse for f in factor]
        for h in range(hc):
            here = pl.ds(j * wide + h * HD, HD)
            total = acc[pl.ds(first, count), :, here].reshape(r, HD) * factor[0][:, h : h + 1]
            for f, ref in zip(factor[1:], parts):
                total = total + ref[:, :, here].astype(jnp.float32).reshape(r, HD) * f[:, h : h + 1]
            if last:
                o_ref[:, pl.ds(j * width + h * HD, HD)] = total.astype(jnp.bfloat16)
            else:
                acc[pl.ds(first, count), :, here] = total.reshape(count, tok, HD)
        if not last:
            fused = jnp.where(lane < HALF, top, jnp.where(lane < 2 * HALF, mass, 0.0))
            acc[pl.ds(first, count), :, at] = fused.reshape(count, tok, LANES)

    def scatter_c(j):
        return [
            remote(send_c.at[k, :, :, wcols(j)], recv_c.at[k, :, :, wcols(j)], rs_sem, rr_sem, j, na + nb + k)
            for k in range(nc)
        ]

    def scatter_b(j):
        return [
            remote(send_b.at[k, :, :, wcols(j)], recv_b.at[k, :, :, wcols(j)], rs_sem, rr_sem, j, na + k)
            for k in range(nb)
        ]

    def scatter_a(j):
        return [
            remote(send_a.at[k, :, :, wcols(j)], recv_a.at[k, :, :, wcols(j)], rs_sem, rr_sem, j, k)
            for k in range(na)
        ]

    def stage_0(j):
        if j == 0:
            own.wait()
        for copy in gather_a[j]:
            copy.wait_recv()
        for copy in gather_b(j):
            copy.start()

    def stage_1(j):
        for copy in gather_b(j):
            copy.wait_recv()
        for copy in gather_c(j):
            copy.start()

    def stage_2(j):
        for copy in gather_c(j):
            copy.wait_recv()
        for copy in loads[j]:
            copy.wait()
        compute(j)
        for k, copy in enumerate(scatter_c(j)):
            pack(slot(0, 0, c_peers[k]), fa * fb, send_c.at[k], j)
            copy.start()

    def stage_3(j):
        for copy in scatter_c(j):
            copy.wait_recv()
        received = [recv_c.at[k] for k in range(nc)]
        for k, copy in enumerate(scatter_b(j)):
            first = b_peers[k] * fa
            merge(slot(0, b_peers[k], c), fa, [x.at[pl.ds(first, fa)] for x in received], j)
            pack(slot(0, b_peers[k], c), fa, send_b.at[k], j)
            copy.start()
        merge(slot(0, b, c), fa, [x.at[pl.ds(b * fa, fa)] for x in received], j)

    def stage_4(j):
        for copy in scatter_b(j):
            copy.wait_recv()
        merge(slot(0, b, c), fa, [recv_b.at[k] for k in range(nb)], j)
        for k, copy in enumerate(scatter_a(j)):
            pack(slot(a_peers[k], b, c), 1, send_a.at[k], j)
            copy.start()

    def stage_5(j):
        for copy in scatter_a(j):
            copy.wait_recv()
        merge(own_slot, 1, [recv_a.at[k] for k in range(na)], j, last=True)

    stages = (stage_0, stage_1, stage_2, stage_3, stage_4, stage_5)
    for step in range(chunks + len(stages) - 1):
        for number, stage in enumerate(stages):
            if 0 <= step - number < chunks:
                stage(step - number)
    for j in range(chunks):
        for group in (gather_a[j], gather_b(j), gather_c(j), scatter_a(j), scatter_b(j), scatter_c(j)):
            for copy in group:
                copy.wait_send()


def per_device(queries, new_keys, new_values, cache_keys, cache_values, victims):
    members = lax.axis_size("seq")
    dims = fa, fb, fc = factors(members)
    tok, columns = queries.shape
    heads = columns // HD
    chunks = chunks_of(heads)
    rows = cache_keys.shape[0]
    keys = rows + -(-2 * tok // LANES) * LANES
    total = columns + chunks * LANES
    peers = fa + fb + fc - 3
    bf16 = jnp.bfloat16
    vmem = pl.BlockSpec(memory_space=pltpu.VMEM)
    hbm = pl.BlockSpec(memory_space=pl.ANY)
    return pl.pallas_call(
        functools.partial(kernel, dims, chunks),
        out_shape=jax.ShapeDtypeStruct((tok, columns), bf16),
        in_specs=[vmem, vmem, vmem, vmem, hbm, hbm],
        out_specs=vmem,
        scratch_shapes=[
            pltpu.VMEM((members, tok, columns), bf16),
            pltpu.VMEM((keys, columns), bf16),
            pltpu.VMEM((keys, columns), bf16),
            pltpu.VMEM((members, tok, total), jnp.float32),
            pltpu.VMEM((max(1, fc - 1), fa * fb, tok, total), bf16),
            pltpu.VMEM((max(1, fc - 1), fa * fb, tok, total), bf16),
            pltpu.VMEM((max(1, fb - 1), fa, tok, total), bf16),
            pltpu.VMEM((max(1, fb - 1), fa, tok, total), bf16),
            pltpu.VMEM((max(1, fa - 1), 1, tok, total), bf16),
            pltpu.VMEM((max(1, fa - 1), 1, tok, total), bf16),
            pltpu.SemaphoreType.DMA((chunks, 2)),
            pltpu.SemaphoreType.DMA,
            pltpu.SemaphoreType.DMA((chunks, peers)),
            pltpu.SemaphoreType.DMA((chunks, peers)),
            pltpu.SemaphoreType.DMA((chunks, peers)),
            pltpu.SemaphoreType.DMA((chunks, peers)),
        ],
        compiler_params=pltpu.CompilerParams(
            collective_id=0, has_side_effects=True, vmem_limit_bytes=60 * 1024 * 1024
        ),
    )(queries, new_keys, new_values, victims.reshape(1, -1), cache_keys, cache_values)


def solution(mesh):
    row = P(("groups", "seq"), None)
    return jax.shard_map(
        per_device,
        mesh=mesh,
        in_specs=(row, row, row, row, row, P("groups")),
        out_specs=row,
        check_vma=False,
    )
```

```python
import functools
import math

import jax
import jax.numpy as jnp
from jax import lax
from jax.experimental import pallas as pl
from jax.experimental.pallas import tpu as pltpu
from jax.sharding import PartitionSpec as P

HD = 128
BLK = 128
LANES = 128
HALF = 32
ROW_TILE = 128
OFFSETS = (0.0, 5.0, 7.3, 9.0, 12.0, 16.0)
STEP = 5.0


def factors(members):
    fc = 2 if members % 2 == 0 else 1
    rest = members // fc
    fa = rest
    for cand in range(1, rest + 1):
        if rest % cand == 0 and cand * cand >= rest:
            fa = cand
            break
    return fa, rest // fa, fc


def chunks_of(heads):
    for count in (4, 5, 2, 3):
        if heads % count == 0 and heads // count <= HALF:
            return count
    return 1 if heads <= HALF else heads


def kernel(
    dims, chunks, q_hbm, nk_hbm, nv_hbm, vic_hbm, ck_ref, cv_ref, o_ref,
    nk_ref, nv_ref, vic_ref, qall, kbuf, vbuf, acc, send_c, recv_c, send_b, recv_b, send_a, recv_a,
    load_sem, small_sem, gs_sem, gr_sem, rs_sem, rr_sem,
):
    fa, fb, fc = dims
    members = fa * fb * fc
    tok, columns = q_hbm.shape
    heads = columns // HD
    hc = heads // chunks
    width = hc * HD
    wide = width + LANES
    rows = ck_ref.shape[0]
    keys = kbuf.shape[0]
    block_count = rows // BLK
    exponent = math.log2(math.e) / math.sqrt(HD)

    me = lax.axis_index("seq")
    c = lax.rem(me, fc)
    b = lax.rem(lax.div(me, fc), fb)
    a = lax.div(me, fc * fb)

    def index(a_, b_, c_):
        return (a_ * fb + b_) * fc + c_

    def slot(a_, b_, c_):
        return (c_ * fb + b_) * fa + a_

    def partners(x, size):
        if size & (size - 1):
            return [lax.rem(x + d, size) for d in range(1, size)], [
                lax.rem(x + size - d, size) for d in range(1, size)
            ]
        found = []
        for d in range(1, size):
            y = x
            bit = 1
            while bit <= d:
                if d & bit:
                    y = y + bit - 2 * bit * lax.rem(lax.div(y, bit), 2)
                bit *= 2
            found.append(y)
        return found, found

    a_peers, a_from = partners(a, fa)
    b_peers, b_from = partners(b, fb)
    c_peers, c_from = partners(c, fc)
    devices = (
        [index(p, b, c) for p in a_peers]
        + [index(a, p, c) for p in b_peers]
        + [index(a, b, p) for p in c_peers]
    )
    na, nb, nc = fa - 1, fb - 1, fc - 1

    def cols(j):
        return pl.ds(j * width, width)

    def wcols(j):
        return pl.ds(j * wide, wide)

    barrier = pltpu.get_barrier_semaphore()
    for dev in devices:
        pl.semaphore_signal(
            barrier, inc=1, device_id={"seq": dev}, device_id_type=pl.DeviceIdType.MESH
        )

    loads = []
    for j in range(chunks):
        pair = (
            pltpu.make_async_copy(
                ck_ref.at[:, cols(j)], kbuf.at[pl.ds(0, rows), cols(j)], load_sem.at[j, 0]
            ),
            pltpu.make_async_copy(
                cv_ref.at[:, cols(j)], vbuf.at[pl.ds(0, rows), cols(j)], load_sem.at[j, 1]
            ),
        )
        loads.append(pair)
    own_slot = slot(a, b, c)
    own = pltpu.make_async_copy(q_hbm, qall.at[own_slot], small_sem.at[0])
    small = [
        pltpu.make_async_copy(nk_hbm, nk_ref, small_sem.at[1]),
        pltpu.make_async_copy(nv_hbm, nv_ref, small_sem.at[2]),
        pltpu.make_async_copy(vic_hbm, vic_ref, small_sem.at[3]),
    ]
    own.start()
    for copy in small:
        copy.start()
    for pair in loads:
        pair[0].start()
        pair[1].start()

    def remote(src, dst, sems, recvs, j, k, target):
        return pltpu.make_async_remote_copy(
            src_ref=src,
            dst_ref=dst,
            send_sem=sems.at[j, k],
            recv_sem=recvs.at[j, k],
            device_id={"seq": target},
            device_id_type=pl.DeviceIdType.MESH,
        )

    def gather(src, j, k, target):
        return remote(src, src, gs_sem, gr_sem, j, k, target)

    def gather_a(j):
        src = qall.at[own_slot, :, cols(j)]
        return [gather(src, j, k, devices[k]) for k in range(na)]

    def gather_b(j, source):
        block = own_slot if source == 0 else slot(a_from[source - 1], b, c)
        src = qall.at[block, :, cols(j)]
        return [gather(src, j, na + source * nb + k, devices[na + k]) for k in range(nb)]

    def gather_c(j, column):
        at_b = b if column == 0 else b_from[column - 1]
        src = qall.at[pl.ds(slot(0, at_b, c), fa), :, cols(j)]
        return [
            gather(src, j, na + fa * nb + column * nc + k, devices[na + nb + k]) for k in range(nc)
        ]

    own.wait()
    pl.semaphore_wait(barrier, len(devices))
    for j in range(chunks):
        for copy in gather_a(j):
            copy.start()
        for copy in gather_b(j, 0):
            copy.start()
    for copy in small:
        copy.wait()

    pad16 = 2 * tok - tok
    for src, dst in ((nk_ref, kbuf), (nv_ref, vbuf)):
        fresh = src[...].astype(jnp.float32)
        dst[pl.ds(rows, 2 * tok), :] = jnp.concatenate(
            [fresh, jnp.zeros((pad16, columns), jnp.float32)], axis=0
        ).astype(jnp.bfloat16)
        dst[pl.ds(rows + 2 * tok, keys - rows - 2 * tok), :] = jnp.zeros(
            (keys - rows - 2 * tok, columns), jnp.bfloat16
        )

    victims = vic_ref[...]
    pieces = []
    for k in range(block_count):
        hit = jnp.where(victims == me * block_count + k, 1.0, 0.0)
        hit = jnp.max(hit, axis=1, keepdims=True)
        pieces.append(jnp.broadcast_to(hit, (1, BLK)) * -1e30)
    tail = lax.broadcasted_iota(jnp.int32, (1, keys - rows), 1)
    pieces.append(jnp.where(tail < tok, 0.0, -1e30))
    bias = jnp.concatenate(pieces, axis=1)

    tile_slots = max(1, min(members, ROW_TILE // tok))
    tiles = members // tile_slots

    def lane_of(r):
        return lax.broadcasted_iota(jnp.int32, (r, LANES), 1)

    def compute(j):
        def tile(t):
            first = t * tile_slots
            r = tile_slots * tok
            lane = lane_of(r)

            def head(h, stats):
                col = pl.multiple_of(j * width + h * HD, HD)
                q = qall[pl.ds(first, tile_slots), :, pl.ds(col, HD)]
                q = q.astype(jnp.float32).reshape(r, HD).astype(jnp.bfloat16)
                s = lax.dot_general(
                    q, kbuf[:, pl.ds(col, HD)], (((1,), (1,)), ((), ())),
                    preferred_element_type=jnp.float32,
                )
                s = s * exponent + bias
                top = jnp.max(s, axis=1, keepdims=True)
                top = top.astype(jnp.bfloat16).astype(jnp.float32)
                e = jnp.exp2(s - top)
                mass = jnp.sum(e, axis=1, keepdims=True)
                out = jnp.dot(
                    e.astype(jnp.bfloat16), vbuf[:, pl.ds(col, HD)],
                    preferred_element_type=jnp.float32,
                )
                at = pl.multiple_of(j * wide + h * HD, HD)
                acc[pl.ds(first, tile_slots), :, pl.ds(at, HD)] = out.reshape(tile_slots, tok, HD)
                stats = jnp.where(lane == h, top, stats)
                return jnp.where(lane == h + HALF, mass, stats)

            stats = lax.fori_loop(
                0, hc, head, jnp.zeros((r, LANES), jnp.float32), unroll=tiles == 1
            )
            acc[pl.ds(first, tile_slots), :, pl.ds(j * wide + width, LANES)] = stats.reshape(
                tile_slots, tok, LANES
            )

        if tiles == 1:
            tile(0)
        else:
            pl.loop(0, tiles)(tile)

    def encode(stats):
        high = stats.astype(jnp.bfloat16).astype(jnp.float32)
        return (high + pltpu.roll(stats - high, HALF, 1)).astype(jnp.bfloat16)

    def decode(stats):
        low = pltpu.roll(stats, LANES - HALF, 1)
        return stats + jnp.where(lane_of(stats.shape[0]) < HALF, 0.0, low)

    def pack(first, count, buf, j):
        r = count * tok
        buf[:, :, cols_w(j, width)] = acc[pl.ds(first, count), :, cols_w(j, width)].astype(
            jnp.bfloat16
        )
        stats = acc[pl.ds(first, count), :, pl.ds(j * wide + width, LANES)].reshape(r, LANES)
        buf[:, :, pl.ds(j * wide + width, LANES)] = encode(stats).reshape(count, tok, LANES)

    def cols_w(j, w):
        return pl.ds(j * wide, w)

    def merge(first, count, parts, j, last=False):
        r = count * tok
        at = pl.ds(j * wide + width, LANES)
        lane = lane_of(r)
        stats = [acc[pl.ds(first, count), :, at].reshape(r, LANES)]
        for ref in parts:
            stats.append(decode(ref[:, :, at].astype(jnp.float32).reshape(r, LANES)))
        top = functools.reduce(jnp.maximum, stats)
        factor = [jnp.exp2(s - top) for s in stats]
        mass = sum(pltpu.roll(f, HALF, 1) * s for f, s in zip(factor, stats))
        if last:
            inverse = pltpu.roll(1.0 / jnp.where(lane < HALF, 1.0, mass), LANES - HALF, 1)
            factor = [f * inverse for f in factor]
        for h in range(hc):
            here = pl.ds(j * wide + h * HD, HD)
            total = acc[pl.ds(first, count), :, here].reshape(r, HD) * factor[0][:, h : h + 1]
            for f, ref in zip(factor[1:], parts):
                total = total + ref[:, :, here].astype(jnp.float32).reshape(r, HD) * f[:, h : h + 1]
            if last:
                o_ref[:, pl.ds(j * width + h * HD, HD)] = total.astype(jnp.bfloat16)
            else:
                acc[pl.ds(first, count), :, here] = total.reshape(count, tok, HD)
        if not last:
            fused = jnp.where(lane < HALF, top, jnp.where(lane < 2 * HALF, mass, 0.0))
            acc[pl.ds(first, count), :, at] = fused.reshape(count, tok, LANES)

    def scatter_c(j):
        return [
            remote(
                send_c.at[k, :, :, wcols(j)], recv_c.at[k, :, :, wcols(j)], rs_sem, rr_sem, j, na + nb + k,
                devices[na + nb + k],
            )
            for k in range(nc)
        ]

    def scatter_b(j):
        return [
            remote(
                send_b.at[k, :, :, wcols(j)], recv_b.at[k, :, :, wcols(j)], rs_sem, rr_sem, j, na + k,
                devices[na + k],
            )
            for k in range(nb)
        ]

    def scatter_a(j):
        return [
            remote(
                send_a.at[k, :, :, wcols(j)], recv_a.at[k, :, :, wcols(j)], rs_sem, rr_sem, j, k,
                devices[k],
            )
            for k in range(na)
        ]

    def stage_0(j):
        for source in range(1, fa):
            gather_a(j)[source - 1].wait_recv()
            for copy in gather_b(j, source):
                copy.start()
        for copy in gather_c(j, 0):
            copy.start()

    def stage_1(j):
        for column in range(1, fb):
            for source in range(fa):
                gather_b(j, source)[column - 1].wait_recv()
            for copy in gather_c(j, column):
                copy.start()

    def stage_2(j):
        for column in range(fb):
            for copy in gather_c(j, column):
                copy.wait_recv()
        for copy in loads[j]:
            copy.wait()
        compute(j)
        for k, copy in enumerate(scatter_c(j)):
            pack(slot(0, 0, c_peers[k]), fa * fb, send_c.at[k], j)
            copy.start()

    def stage_3(j):
        for copy in scatter_c(j):
            copy.wait_recv()
        received = [recv_c.at[k] for k in range(nc)]
        for k, copy in enumerate(scatter_b(j)):
            first = b_peers[k] * fa
            merge(slot(0, b_peers[k], c), fa, [x.at[pl.ds(first, fa)] for x in received], j)
            pack(slot(0, b_peers[k], c), fa, send_b.at[k], j)
            copy.start()
        merge(slot(0, b, c), fa, [x.at[pl.ds(b * fa, fa)] for x in received], j)

    def stage_4(j):
        for copy in scatter_b(j):
            copy.wait_recv()
        merge(slot(0, b, c), fa, [recv_b.at[k] for k in range(nb)], j)
        for k, copy in enumerate(scatter_a(j)):
            pack(slot(a_peers[k], b, c), 1, send_a.at[k], j)
            copy.start()

    def stage_5(j):
        for copy in scatter_a(j):
            copy.wait_recv()
        merge(own_slot, 1, [recv_a.at[k] for k in range(na)], j, last=True)

    stages = (stage_0, stage_1, stage_2, stage_3, stage_4, stage_5)
    order = sorted(
        (OFFSETS[number] + j * STEP / chunks, number, j)
        for number in range(len(stages))
        for j in range(chunks)
    )
    for _, number, j in order:
        stages[number](j)
    for j in range(chunks):
        groups = [gather_a(j), scatter_a(j), scatter_b(j), scatter_c(j)]
        groups += [gather_b(j, source) for source in range(fa)]
        groups += [gather_c(j, column) for column in range(fb)]
        for group in groups:
            for copy in group:
                copy.wait_send()


def per_device(queries, new_keys, new_values, cache_keys, cache_values, victims):
    members = lax.axis_size("seq")
    dims = fa, fb, fc = factors(members)
    tok, columns = queries.shape
    heads = columns // HD
    chunks = chunks_of(heads)
    rows = cache_keys.shape[0]
    keys = rows + -(-2 * tok // LANES) * LANES
    total = columns + chunks * LANES
    peers = fa + fb + fc - 3
    copies = fa - 1 + fa * (fb - 1) + fb * (fc - 1)
    bf16 = jnp.bfloat16
    vmem = pl.BlockSpec(memory_space=pltpu.VMEM)
    hbm = pl.BlockSpec(memory_space=pl.ANY)
    return pl.pallas_call(
        functools.partial(kernel, dims, chunks),
        out_shape=jax.ShapeDtypeStruct((tok, columns), bf16),
        in_specs=[hbm] * 6,
        out_specs=vmem,
        scratch_shapes=[
            pltpu.VMEM((tok, columns), bf16),
            pltpu.VMEM((tok, columns), bf16),
            pltpu.VMEM((1, victims.shape[0]), jnp.int32),
            pltpu.VMEM((members, tok, columns), bf16),
            pltpu.VMEM((keys, columns), bf16),
            pltpu.VMEM((keys, columns), bf16),
            pltpu.VMEM((members, tok, total), jnp.float32),
            pltpu.VMEM((max(1, fc - 1), fa * fb, tok, total), bf16),
            pltpu.VMEM((max(1, fc - 1), fa * fb, tok, total), bf16),
            pltpu.VMEM((max(1, fb - 1), fa, tok, total), bf16),
            pltpu.VMEM((max(1, fb - 1), fa, tok, total), bf16),
            pltpu.VMEM((max(1, fa - 1), 1, tok, total), bf16),
            pltpu.VMEM((max(1, fa - 1), 1, tok, total), bf16),
            pltpu.SemaphoreType.DMA((chunks, 2)),
            pltpu.SemaphoreType.DMA((4,)),
            pltpu.SemaphoreType.DMA((chunks, copies)),
            pltpu.SemaphoreType.DMA((chunks, copies)),
            pltpu.SemaphoreType.DMA((chunks, peers)),
            pltpu.SemaphoreType.DMA((chunks, peers)),
        ],
        compiler_params=pltpu.CompilerParams(
            collective_id=0, has_side_effects=True, vmem_limit_bytes=60 * 1024 * 1024
        ),
    )(queries, new_keys, new_values, victims.reshape(1, -1), cache_keys, cache_values)


def solution(mesh):
    row = P(("groups", "seq"), None)
    return jax.shard_map(
        per_device,
        mesh=mesh,
        in_specs=(row, row, row, row, row, P("groups")),
        out_specs=row,
        check_vma=False,
    )
```

```python
import functools
import math

import jax
import jax.numpy as jnp
from jax import lax
from jax.experimental import pallas as pl
from jax.experimental.pallas import tpu as pltpu
from jax.sharding import PartitionSpec as P

HD = 128
BLK = 128
LANES = 128
HALF = 32
ROW_TILE = 128
OFFSETS = (0.0, 5.0, 7.3, 9.0, 12.0, 16.0)
STEP = 5.0


def factors(members):
    fc = 2 if members % 2 == 0 else 1
    rest = members // fc
    fa = rest
    for cand in range(1, rest + 1):
        if rest % cand == 0 and cand * cand >= rest:
            fa = cand
            break
    return fa, rest // fa, fc


def chunks_of(heads):
    for count in (4, 5, 2, 3):
        if heads % count == 0 and heads // count <= HALF:
            return count
    return 1 if heads <= HALF else heads


def kernel(
    dims, chunks, q_hbm, nk_hbm, nv_hbm, vic_hbm, ck_ref, cv_ref, o_ref,
    nk_ref, nv_ref, vic_ref, qall, kbuf, vbuf, acc, send_c, recv_c, send_b, recv_b, send_a, recv_a,
    load_sem, small_sem, gs_sem, gr_sem, rs_sem, rr_sem,
):
    fa, fb, fc = dims
    members = fa * fb * fc
    tok, columns = q_hbm.shape
    heads = columns // HD
    hc = heads // chunks
    width = hc * HD
    wide = width + LANES
    rows = ck_ref.shape[0]
    keys = kbuf.shape[0]
    block_count = rows // BLK
    exponent = math.log2(math.e) / math.sqrt(HD)

    me = lax.axis_index("seq")
    c = lax.rem(me, fc)
    b = lax.rem(lax.div(me, fc), fb)
    a = lax.div(me, fc * fb)

    def index(a_, b_, c_):
        return (a_ * fb + b_) * fc + c_

    def slot(a_, b_, c_):
        return (c_ * fb + b_) * fa + a_

    def partners(x, size):
        if size & (size - 1):
            return [lax.rem(x + d, size) for d in range(1, size)], [
                lax.rem(x + size - d, size) for d in range(1, size)
            ]
        found = []
        for d in range(1, size):
            y = x
            bit = 1
            while bit <= d:
                if d & bit:
                    y = y + bit - 2 * bit * lax.rem(lax.div(y, bit), 2)
                bit *= 2
            found.append(y)
        return found, found

    a_peers, a_from = partners(a, fa)
    b_peers, b_from = partners(b, fb)
    c_peers, c_from = partners(c, fc)
    devices = (
        [index(p, b, c) for p in a_peers]
        + [index(a, p, c) for p in b_peers]
        + [index(a, b, p) for p in c_peers]
    )
    na, nb, nc = fa - 1, fb - 1, fc - 1

    def cols(j):
        return pl.ds(j * width, width)

    def wcols(j):
        return pl.ds(j * wide, wide)

    barrier = pltpu.get_barrier_semaphore()
    for dev in devices:
        pl.semaphore_signal(
            barrier, inc=1, device_id={"seq": dev}, device_id_type=pl.DeviceIdType.MESH
        )

    loads = []
    for j in range(chunks):
        pair = (
            pltpu.make_async_copy(
                ck_ref.at[:, cols(j)], kbuf.at[pl.ds(0, rows), cols(j)], load_sem.at[j, 0]
            ),
            pltpu.make_async_copy(
                cv_ref.at[:, cols(j)], vbuf.at[pl.ds(0, rows), cols(j)], load_sem.at[j, 1]
            ),
        )
        loads.append(pair)
    own_slot = slot(a, b, c)
    own = pltpu.make_async_copy(q_hbm, qall.at[own_slot], small_sem.at[0])
    small = [
        pltpu.make_async_copy(nk_hbm, nk_ref, small_sem.at[1]),
        pltpu.make_async_copy(nv_hbm, nv_ref, small_sem.at[2]),
        pltpu.make_async_copy(vic_hbm, vic_ref, small_sem.at[3]),
    ]
    own.start()
    for copy in small:
        copy.start()
    for pair in loads:
        pair[0].start()
        pair[1].start()

    def remote(src, dst, sems, recvs, j, k, target):
        return pltpu.make_async_remote_copy(
            src_ref=src,
            dst_ref=dst,
            send_sem=sems.at[j, k],
            recv_sem=recvs.at[j, k],
            device_id={"seq": target},
            device_id_type=pl.DeviceIdType.MESH,
        )

    def gather(src, j, k, target):
        return remote(src, src, gs_sem, gr_sem, j, k, target)

    def gather_a(j):
        src = qall.at[own_slot, :, cols(j)]
        return [gather(src, j, k, devices[k]) for k in range(na)]

    def gather_b(j, source):
        block = own_slot if source == 0 else slot(a_from[source - 1], b, c)
        src = qall.at[block, :, cols(j)]
        return [gather(src, j, na + source * nb + k, devices[na + k]) for k in range(nb)]

    def gather_c(j, column):
        at_b = b if column == 0 else b_from[column - 1]
        src = qall.at[pl.ds(slot(0, at_b, c), fa), :, cols(j)]
        return [
            gather(src, j, na + fa * nb + column * nc + k, devices[na + nb + k]) for k in range(nc)
        ]

    own.wait()
    pl.semaphore_wait(barrier, len(devices))
    for j in range(chunks):
        for copy in gather_a(j):
            copy.start()
        for copy in gather_b(j, 0):
            copy.start()
    for copy in small:
        copy.wait()

    pad16 = 2 * tok - tok
    for src, dst in ((nk_ref, kbuf), (nv_ref, vbuf)):
        fresh = src[...].astype(jnp.float32)
        dst[pl.ds(rows, 2 * tok), :] = jnp.concatenate(
            [fresh, jnp.zeros((pad16, columns), jnp.float32)], axis=0
        ).astype(jnp.bfloat16)
        dst[pl.ds(rows + 2 * tok, keys - rows - 2 * tok), :] = jnp.zeros(
            (keys - rows - 2 * tok, columns), jnp.bfloat16
        )

    victims = vic_ref[...]
    pieces = []
    for k in range(block_count):
        hit = jnp.where(victims == me * block_count + k, 1.0, 0.0)
        hit = jnp.max(hit, axis=1, keepdims=True)
        pieces.append(jnp.broadcast_to(hit, (1, BLK)) * -1e30)
    tail = lax.broadcasted_iota(jnp.int32, (1, keys - rows), 1)
    pieces.append(jnp.where(tail < tok, 0.0, -1e30))
    bias = jnp.concatenate(pieces, axis=1)

    tile_slots = max(1, min(members, ROW_TILE // tok))
    tiles = members // tile_slots

    def lane_of(r):
        return lax.broadcasted_iota(jnp.int32, (r, LANES), 1)

    def compute(j):
        def tile(t):
            first = t * tile_slots
            r = tile_slots * tok
            lane = lane_of(r)

            def scores(h):
                col = j * width + h * HD
                col = col if isinstance(col, int) else pl.multiple_of(col, HD)
                q = qall[pl.ds(first, tile_slots), :, pl.ds(col, HD)]
                q = q.astype(jnp.float32).reshape(r, HD).astype(jnp.bfloat16)
                return lax.dot_general(
                    q, kbuf[:, pl.ds(col, HD)], (((1,), (1,)), ((), ())),
                    preferred_element_type=jnp.float32,
                )

            def head(h, stats, s):
                col = j * width + h * HD
                col = col if isinstance(col, int) else pl.multiple_of(col, HD)
                s = s * exponent + bias
                top = jnp.max(s, axis=1, keepdims=True)
                top = top.astype(jnp.bfloat16).astype(jnp.float32)
                e = jnp.exp2(s - top)
                mass = jnp.sum(e, axis=1, keepdims=True)
                out = jnp.dot(
                    e.astype(jnp.bfloat16), vbuf[:, pl.ds(col, HD)],
                    preferred_element_type=jnp.float32,
                )
                at = j * wide + h * HD
                at = at if isinstance(at, int) else pl.multiple_of(at, HD)
                acc[pl.ds(first, tile_slots), :, pl.ds(at, HD)] = out.reshape(tile_slots, tok, HD)
                stats = jnp.where(lane == h, top, stats)
                return jnp.where(lane == h + HALF, mass, stats)

            stats = jnp.zeros((r, LANES), jnp.float32)
            if tiles == 1:
                ahead = scores(0)
                for h in range(hc):
                    now, ahead = ahead, scores(h + 1) if h + 1 < hc else None
                    stats = head(h, stats, now)
            else:
                stats = lax.fori_loop(0, hc, lambda h, st: head(h, st, scores(h)), stats)
            acc[pl.ds(first, tile_slots), :, pl.ds(j * wide + width, LANES)] = stats.reshape(
                tile_slots, tok, LANES
            )

        if tiles == 1:
            tile(0)
        else:
            pl.loop(0, tiles)(tile)

    def encode(stats):
        high = stats.astype(jnp.bfloat16).astype(jnp.float32)
        return (high + pltpu.roll(stats - high, HALF, 1)).astype(jnp.bfloat16)

    def decode(stats):
        low = pltpu.roll(stats, LANES - HALF, 1)
        return stats + jnp.where(lane_of(stats.shape[0]) < HALF, 0.0, low)

    def pack(first, count, buf, j):
        r = count * tok
        buf[:, :, cols_w(j, width)] = acc[pl.ds(first, count), :, cols_w(j, width)].astype(
            jnp.bfloat16
        )
        stats = acc[pl.ds(first, count), :, pl.ds(j * wide + width, LANES)].reshape(r, LANES)
        buf[:, :, pl.ds(j * wide + width, LANES)] = encode(stats).reshape(count, tok, LANES)

    def cols_w(j, w):
        return pl.ds(j * wide, w)

    def merge(first, count, parts, j, last=False):
        r = count * tok
        at = pl.ds(j * wide + width, LANES)
        lane = lane_of(r)
        stats = [acc[pl.ds(first, count), :, at].reshape(r, LANES)]
        for ref in parts:
            stats.append(decode(ref[:, :, at].astype(jnp.float32).reshape(r, LANES)))
        top = functools.reduce(jnp.maximum, stats)
        factor = [jnp.exp2(s - top) for s in stats]
        mass = sum(pltpu.roll(f, HALF, 1) * s for f, s in zip(factor, stats))
        if last:
            inverse = pltpu.roll(1.0 / jnp.where(lane < HALF, 1.0, mass), LANES - HALF, 1)
            factor = [f * inverse for f in factor]
        for h in range(hc):
            here = pl.ds(j * wide + h * HD, HD)
            total = acc[pl.ds(first, count), :, here].reshape(r, HD) * factor[0][:, h : h + 1]
            for f, ref in zip(factor[1:], parts):
                total = total + ref[:, :, here].astype(jnp.float32).reshape(r, HD) * f[:, h : h + 1]
            if last:
                o_ref[:, pl.ds(j * width + h * HD, HD)] = total.astype(jnp.bfloat16)
            else:
                acc[pl.ds(first, count), :, here] = total.reshape(count, tok, HD)
        if not last:
            fused = jnp.where(lane < HALF, top, jnp.where(lane < 2 * HALF, mass, 0.0))
            acc[pl.ds(first, count), :, at] = fused.reshape(count, tok, LANES)

    def scatter_c(j):
        return [
            remote(
                send_c.at[k, :, :, wcols(j)], recv_c.at[k, :, :, wcols(j)], rs_sem, rr_sem, j, na + nb + k,
                devices[na + nb + k],
            )
            for k in range(nc)
        ]

    def scatter_b(j):
        return [
            remote(
                send_b.at[k, :, :, wcols(j)], recv_b.at[k, :, :, wcols(j)], rs_sem, rr_sem, j, na + k,
                devices[na + k],
            )
            for k in range(nb)
        ]

    def scatter_a(j):
        return [
            remote(
                send_a.at[k, :, :, wcols(j)], recv_a.at[k, :, :, wcols(j)], rs_sem, rr_sem, j, k,
                devices[k],
            )
            for k in range(na)
        ]

    def stage_0(j):
        for source in range(1, fa):
            gather_a(j)[source - 1].wait_recv()
            for copy in gather_b(j, source):
                copy.start()
        for copy in gather_c(j, 0):
            copy.start()

    def stage_1(j):
        for column in range(1, fb):
            for source in range(fa):
                gather_b(j, source)[column - 1].wait_recv()
            for copy in gather_c(j, column):
                copy.start()

    def stage_2(j):
        for column in range(fb):
            for copy in gather_c(j, column):
                copy.wait_recv()
        for copy in loads[j]:
            copy.wait()
        compute(j)
        for k, copy in enumerate(scatter_c(j)):
            pack(slot(0, 0, c_peers[k]), fa * fb, send_c.at[k], j)
            copy.start()

    def stage_3(j):
        for copy in scatter_c(j):
            copy.wait_recv()
        received = [recv_c.at[k] for k in range(nc)]
        for k, copy in enumerate(scatter_b(j)):
            first = b_peers[k] * fa
            merge(slot(0, b_peers[k], c), fa, [x.at[pl.ds(first, fa)] for x in received], j)
            pack(slot(0, b_peers[k], c), fa, send_b.at[k], j)
            copy.start()
        merge(slot(0, b, c), fa, [x.at[pl.ds(b * fa, fa)] for x in received], j)

    def stage_4(j):
        for copy in scatter_b(j):
            copy.wait_recv()
        merge(slot(0, b, c), fa, [recv_b.at[k] for k in range(nb)], j)
        for k, copy in enumerate(scatter_a(j)):
            pack(slot(a_peers[k], b, c), 1, send_a.at[k], j)
            copy.start()

    def stage_5(j):
        for copy in scatter_a(j):
            copy.wait_recv()
        merge(own_slot, 1, [recv_a.at[k] for k in range(na)], j, last=True)

    stages = (stage_0, stage_1, stage_2, stage_3, stage_4, stage_5)
    order = sorted(
        (OFFSETS[number] + j * STEP / chunks, number, j)
        for number in range(len(stages))
        for j in range(chunks)
    )
    for _, number, j in order:
        stages[number](j)
    for j in range(chunks):
        groups = [gather_a(j), scatter_a(j), scatter_b(j), scatter_c(j)]
        groups += [gather_b(j, source) for source in range(fa)]
        groups += [gather_c(j, column) for column in range(fb)]
        for group in groups:
            for copy in group:
                copy.wait_send()


def per_device(queries, new_keys, new_values, cache_keys, cache_values, victims):
    members = lax.axis_size("seq")
    dims = fa, fb, fc = factors(members)
    tok, columns = queries.shape
    heads = columns // HD
    chunks = chunks_of(heads)
    rows = cache_keys.shape[0]
    keys = rows + -(-2 * tok // LANES) * LANES
    total = columns + chunks * LANES
    peers = fa + fb + fc - 3
    copies = fa - 1 + fa * (fb - 1) + fb * (fc - 1)
    bf16 = jnp.bfloat16
    vmem = pl.BlockSpec(memory_space=pltpu.VMEM)
    hbm = pl.BlockSpec(memory_space=pl.ANY)
    return pl.pallas_call(
        functools.partial(kernel, dims, chunks),
        out_shape=jax.ShapeDtypeStruct((tok, columns), bf16),
        in_specs=[hbm] * 6,
        out_specs=vmem,
        scratch_shapes=[
            pltpu.VMEM((tok, columns), bf16),
            pltpu.VMEM((tok, columns), bf16),
            pltpu.VMEM((1, victims.shape[0]), jnp.int32),
            pltpu.VMEM((members, tok, columns), bf16),
            pltpu.VMEM((keys, columns), bf16),
            pltpu.VMEM((keys, columns), bf16),
            pltpu.VMEM((members, tok, total), jnp.float32),
            pltpu.VMEM((max(1, fc - 1), fa * fb, tok, total), bf16),
            pltpu.VMEM((max(1, fc - 1), fa * fb, tok, total), bf16),
            pltpu.VMEM((max(1, fb - 1), fa, tok, total), bf16),
            pltpu.VMEM((max(1, fb - 1), fa, tok, total), bf16),
            pltpu.VMEM((max(1, fa - 1), 1, tok, total), bf16),
            pltpu.VMEM((max(1, fa - 1), 1, tok, total), bf16),
            pltpu.SemaphoreType.DMA((chunks, 2)),
            pltpu.SemaphoreType.DMA((4,)),
            pltpu.SemaphoreType.DMA((chunks, copies)),
            pltpu.SemaphoreType.DMA((chunks, copies)),
            pltpu.SemaphoreType.DMA((chunks, peers)),
            pltpu.SemaphoreType.DMA((chunks, peers)),
        ],
        compiler_params=pltpu.CompilerParams(
            collective_id=0, has_side_effects=True, vmem_limit_bytes=60 * 1024 * 1024
        ),
    )(queries, new_keys, new_values, victims.reshape(1, -1), cache_keys, cache_values)


def solution(mesh):
    row = P(("groups", "seq"), None)
    return jax.shard_map(
        per_device,
        mesh=mesh,
        in_specs=(row, row, row, row, row, P("groups")),
        out_specs=row,
        check_vma=False,
    )
```
